512 devices in a mesh: section: 16 (over z, core), mp: 32 (over y, x).
Axes of the slice: x: 4, y: 8, z: 8, core: 2. Of those that a mesh axis runs over, the one named last changes fastest.
Arguments:
- hidden_in: bfloat16 [16, 384, 8192], P('section', None, 'mp'), may hold values from -6 to 6
- positions: int32 [16, 384], replicated, may hold values from 0 to 383, as said below
- routed_rows: int32 [8, 16, 48], replicated, may hold values from 0 to 383, as said below
- gain: bfloat16 [16, 8192], P('section'), may hold values from 0.25 to 1.75
- router: bfloat16 [16, 8192], P('section'), may hold values from -0.0625 to 0.0625
- w_query: bfloat16 [16, 8192, 4096], P('section', None, 'mp')
- w_key: bfloat16 [16, 8192, 512], P('section', None, 'mp')
- w_value: bfloat16 [16, 8192, 512], P('section', None, 'mp'), may hold values from -0.0625 to 0.0625
- w_out: bfloat16 [16, 4096, 8192], P('section', None, 'mp'), may hold values from -0.09375 to 0.09375
Outputs:
- hidden_out: bfloat16 [16, 384, 8192], P('section', None, 'mp')
The draws below stay inside these ranges and needn't reach their ends.
Inputs may be any that keep to these rules, and one draw needn't show every extreme that they name: Each micro-batch is a pack of documents; a token's position counts from its document's first token, so positions restart at 0 at every document start and rise by one otherwise; in every draw one micro-batch is a single document. `routed_rows`: each of the 8 x 16 lists holds 48 distinct token rows of its micro-batch in ascending order.
All inputs are finite; a program needn't handle non-finite values.
Results may differ from the reference program's by a relative error of at most 0.008.
Values may be sent and summed in bfloat16 or wider, within the bound.
A program may use at most 64 MiB of HBM per device.

```python
import math
import jax
import jax.numpy as jnp
from jax import lax

D = 8192
HEADS = 32
KV_HEADS = 4
HEAD_DIM = 128
TOK = 384
TICKS = 8
GROUP = 8
ROUTED = 48
SECTIONS = 16


def common_query(key):
    spread = jax.random.normal(jax.random.fold_in(key, 11), (SECTIONS, D, HEADS * HEAD_DIM), jnp.float32)
    return spread * D ** (-0.5)


def draw_w_query(key, part):
    return common_query(key).astype(jnp.bfloat16)


def draw_w_key(key, part):
    jitter = jax.random.normal(jax.random.fold_in(key, 13), (SECTIONS, D, KV_HEADS, HEAD_DIM), jnp.float32) * D ** (-0.5)
    result = jitter
    mixed = jnp.transpose(result.reshape(SECTIONS, D, KV_HEADS, HEAD_DIM // 2, 2), (0, 1, 3, 2, 4))
    return mixed.reshape(SECTIONS, D, KV_HEADS * HEAD_DIM).astype(jnp.bfloat16)


def draw_positions(key, part):
    start_bits = jax.random.randint(jax.random.fold_in(key, 3), (SECTIONS, TOK), 0, 48)
    single_doc = jax.random.randint(jax.random.fold_in(key, 4), (), 0, SECTIONS)
    starts = (start_bits == 0) & (jnp.arange(SECTIONS, dtype=jnp.int32)[:, None] != single_doc)
    starts = starts.at[:, 0].set(True)
    columns = jnp.broadcast_to(jnp.arange(TOK, dtype=jnp.int32)[None, :], (SECTIONS, TOK))
    marked = jnp.where(starts, columns, 0)
    doc_start = lax.cummax(marked, axis=1)
    return (columns - doc_start).astype(jnp.int32)


def draw_routed_rows(key, part):
    subkeys = jax.random.split(jax.random.fold_in(key, 5), TICKS * SECTIONS)

    def choose(subkey):
        chosen = jax.random.permutation(subkey, TOK)[:ROUTED]
        return jnp.sort(chosen)
    return jax.vmap(choose)(subkeys).reshape(TICKS, SECTIONS, ROUTED).astype(jnp.int32)


def shard_levels(own_key, extent, shards, smallest, top_value):
    level, own = 1.0, jax.random.fold_in(own_key, 6)
    for dim, parts in shards:
        draws = jnp.exp(jax.random.uniform(jax.random.fold_in(own, dim), (parts,), jnp.float32, smallest / len(shards), top_value / len(shards)))
        level = level * jnp.repeat(draws, extent[dim] // parts).reshape([-1 if axis == dim else 1 for axis in range(len(extent))])
    return level


def centred(key, extent, scale, limit, cuts=(), kind=jnp.bfloat16):
    array = scale * jax.random.normal(key, extent, jnp.float32)
    if cuts:
        array = array * shard_levels(key, extent, cuts, -0.22, 0.18)
    return jnp.clip(array, -limit, limit).astype(kind)


def setup_inputs(seed: int = 0) -> dict:
    key_of = jax.random.split(jax.random.key(seed), 10)
    return {
        "hidden_in": centred(key_of[0], (SECTIONS, TOK, D), 1.0, 6.0, ((0, 16), (2, 32))),
        "positions": draw_positions(jax.random.fold_in(key_of[9], 71), 0),
        "routed_rows": draw_routed_rows(jax.random.fold_in(key_of[9], 71), 0),
        "gain": jnp.clip(1.0 + 0.15 * jax.random.normal(key_of[3], (SECTIONS, D), jnp.float32), 0.25, 1.75).astype(jnp.bfloat16),
        "router": centred(key_of[4], (SECTIONS, D), D ** -0.5, 0.0625, ((0, 16),)),
        "w_query": draw_w_query(jax.random.fold_in(key_of[9], 71), 0),
        "w_key": draw_w_key(jax.random.fold_in(key_of[9], 71), 0),
        "w_value": centred(key_of[7], (SECTIONS, D, KV_HEADS * HEAD_DIM), D ** -0.5, 0.0625, ((0, 16), (2, 32))),
        "w_out": centred(key_of[8], (SECTIONS, HEADS * HEAD_DIM, D), (HEADS * HEAD_DIM) ** -0.5, 0.09375, ((0, 16), (2, 32))),
    }


rope_base = 500000.0
norm_epsilon = 1e-05

def turn_pairs(matrix, row_positions, pair_index):
    row_count, col_count = matrix.shape
    paired = matrix.reshape(row_count, col_count // 2, 2)
    frequency = jnp.exp(pair_index.astype(jnp.float32) * (-2.0 * math.log(rope_base) / HEAD_DIM))
    angles = row_positions.astype(jnp.float32)[:, None] * frequency[None, :]
    cosine = jnp.cos(angles)
    sine_value = jnp.sin(angles)
    real_part = paired[:, :, 0]
    imag_part = paired[:, :, 1]
    turned = jnp.stack([real_part * cosine - imag_part * sine_value, real_part * sine_value + imag_part * cosine], axis=2)
    return turned.reshape(row_count, col_count)

def rotate(matrix, row_positions, offset):
    col_count = matrix.shape[1]
    pair_index = (jnp.arange(col_count // 2, dtype=jnp.int32) * 2 + offset) % HEAD_DIM // 2
    return turn_pairs(matrix, row_positions, pair_index)

def rotate_mixed(matrix, row_positions, offset):
    col_count = matrix.shape[1]
    pair_index = (jnp.arange(col_count // 2, dtype=jnp.int32) * 2 + offset) // (2 * KV_HEADS)
    return turn_pairs(matrix, row_positions, pair_index)

def to_heads(block):
    row_count = block.shape[0]
    split = block.reshape(row_count, HEAD_DIM // 2, KV_HEADS, 2)
    return jnp.transpose(split, (0, 2, 1, 3)).reshape(row_count, KV_HEADS, HEAD_DIM)

def visible(token_rows, row_positions):
    causal = token_rows[:, None] >= token_rows[None, :]
    within = token_rows[:, None] - token_rows[None, :] <= row_positions[:, None]
    return causal & within

def attend(query_heads, key_heads, value_heads, allowed):
    scores = jnp.einsum('qhd,khd->hqk', query_heads.astype(jnp.float32), key_heads.astype(jnp.float32)) / math.sqrt(HEAD_DIM)
    scores = jnp.where(allowed[None, :, :], scores, -1e+30)
    maximum = lax.optimization_barrier(jnp.max(scores, axis=2, keepdims=True))
    exponent = jnp.exp(scores - maximum)
    weights = (exponent / lax.optimization_barrier(jnp.sum(exponent, axis=2, keepdims=True))).astype(jnp.bfloat16)
    attended = jnp.einsum('hqk,khd->qhd', weights.astype(jnp.float32), value_heads.astype(jnp.float32))
    return attended.astype(jnp.bfloat16).reshape(query_heads.shape[0], -1)

def section_block(hidden, doc_positions, token_rows, gain_row, router_row, query_weight, key_weight, value_weight, out_weight):
    picked = hidden[token_rows]
    widened = picked.astype(jnp.float32)
    inverse_rms = lax.rsqrt(lax.optimization_barrier(jnp.mean(widened * widened, axis=1, keepdims=True)) + norm_epsilon)
    normed = (widened * inverse_rms * gain_row.astype(jnp.float32)[None, :]).astype(jnp.bfloat16)
    gate = jax.nn.sigmoid(jnp.dot(picked, router_row, preferred_element_type=jnp.float32))
    row_positions = doc_positions[token_rows]
    queries = rotate(jnp.dot(normed, query_weight, preferred_element_type=jnp.float32), row_positions, 0).astype(jnp.bfloat16)
    key_block = rotate_mixed(jnp.dot(normed, key_weight, preferred_element_type=jnp.float32), row_positions, 0).astype(jnp.bfloat16)
    value_block = jnp.dot(normed, value_weight, preferred_element_type=jnp.float32).astype(jnp.bfloat16)
    allowed = visible(token_rows, row_positions)
    query_heads = queries.reshape(ROUTED, HEADS, HEAD_DIM)
    key_heads = jnp.repeat(to_heads(key_block), GROUP, axis=1)
    value_heads = jnp.repeat(to_heads(value_block), GROUP, axis=1)
    attended = attend(query_heads, key_heads, value_heads, allowed)
    update = jnp.dot(attended, out_weight, preferred_element_type=jnp.float32)
    new_rows = (widened + gate[:, None] * update).astype(jnp.bfloat16)
    return hidden.at[token_rows].set(new_rows)

def reference(hidden_in, positions, routed_rows, gain, router, w_query, w_key, w_value, w_out):
    hidden = hidden_in
    for step_number in range(TICKS):
        results = []
        for section_number in range(SECTIONS):
            source = (section_number - step_number) % SECTIONS
            results.append(section_block(hidden[section_number], positions[source], routed_rows[step_number, section_number], gain[section_number], router[section_number], w_query[section_number], w_key[section_number], w_value[section_number], w_out[section_number]))
        stacked = jnp.stack(results)
        hidden = jnp.roll(stacked, 1, axis=0)
    return hidden
```

```python
import functools
import math

import jax
import jax.numpy as jnp
from jax import lax
from jax.experimental import pallas as pl
from jax.experimental.pallas import tpu as pltpu
from jax.sharding import PartitionSpec as P

KV_HEADS = 4
HEAD_DIM = 128
TICKS = 8
GROUP = 8
ROUTED = 48
NX = 4
NY = 8

rope_base = 500000.0
norm_epsilon = 1e-05

MESH = pl.DeviceIdType.MESH
F32 = jnp.float32
BF16 = jnp.bfloat16
ORDER = (0, 1, 7, 2, 6, 3, 5, 4)


def dot(a, b):
    return jnp.dot(a, b, preferred_element_type=F32)


def dot_nt(a, b):
    return lax.dot_general(a, b, (((1,), (1,)), ((), ())), preferred_element_type=F32)


def dot_tn(a, b):
    return lax.dot_general(a, b, (((0,), (0,)), ((), ())), preferred_element_type=F32)


def kernel(
    sections,
    hidden_ref, weight_ref, out_weight_ref, gain_ref, router_ref,
    cos_ref, sin_ref, seen_ref, rows_ref, next_rows_ref,
    o_ref,
    hid, picked, picked_out, blocks, kv_tiles, kv_all, att, att_blocks,
    hid_send, hid_recv, picked_send, picked_recv,
    ys1, yr1, xs1, xr1, rs1, rr1,
    ys3, yr3, xs3, xr3, rs3, rr3,
    kys, kyr, kxs, kxr,
):
    s = lax.axis_index("section")
    m = lax.axis_index("mp")
    x = lax.rem(m, NX)
    y = lax.div(m, NX)
    after = lax.rem(s + 1, sections)
    before = lax.rem(s + sections - 1, sections)

    def at_y(d):
        return lax.rem(y + d + NY, NY)

    def at_x(d):
        return lax.rem(x + d + NX, NX)

    def dev(yy, xx):
        return (s, yy * NX + xx)

    barrier = pltpu.get_barrier_semaphore()
    peers = [dev(at_y(d), x) for d in range(1, NY)] + [dev(y, at_x(d)) for d in range(1, NX)]
    peers += [(after, m), (before, m)]
    for peer in peers:
        pl.semaphore_signal(barrier, inc=1, device_id=peer, device_id_type=MESH)

    def remote(src, dst, send, recv, to):
        return pltpu.make_async_remote_copy(
            src_ref=src, dst_ref=dst, send_sem=send, recv_sem=recv, device_id=to, device_id_type=MESH
        )

    def gather(own, into, sems, consume):
        ys, yr, xs, xr, rs, rr = sems
        right = dev(y, at_x(1))
        left = dev(y, at_x(-1))

        def slot(j, xx):
            return at_y(-j) * NX + xx

        def y_copy(j, source_y):
            return remote(own, into.at[source_y * NX + x], ys.at[j], yr.at[j], dev(at_y(j), x))

        def x_copy(j, way, src, src_x):
            to = right if way == 0 else left
            return remote(src, into.at[slot(j, src_x)], xs.at[2 * j + way], xr.at[2 * j + way], to)

        def r_copy(j, src_x):
            to = right if j % 2 == 0 else left
            block = into.at[slot(j, src_x)]
            return remote(block, block, rs.at[j], rr.at[j], to)

        for j in (4, 3, 5, 2, 6, 1, 7):
            y_copy(j, y).start()
        sent = []
        for t in range(NY + 2):
            if t < NY:
                j = ORDER[t]
                if j == 0:
                    mine = own
                else:
                    y_copy(j, at_y(-j)).wait_recv()
                    mine = into.at[slot(j, x)]
                for way in (0, 1):
                    copy = x_copy(j, way, mine, x)
                    copy.start()
                    sent.append(copy)
                consume(mine, slot(j, x))
            if 1 <= t <= NY:
                j = ORDER[t - 1]
                for way, src_x in ((0, at_x(-1)), (1, at_x(1))):
                    x_copy(j, way, into.at[slot(j, src_x)], src_x).wait_recv()
                    if j % 2 == way:
                        copy = r_copy(j, src_x)
                        copy.start()
                        sent.append(copy)
                    consume(into.at[slot(j, src_x)], slot(j, src_x))
            if t >= 2:
                j = ORDER[t - 2]
                r_copy(j, at_x(2)).wait_recv()
                consume(into.at[slot(j, at_x(2))], slot(j, at_x(2)))

        def finish():
            for j in range(1, NY):
                y_copy(j, y).wait_send()
            for copy in sent:
                copy.wait_send()

        return finish

    hid[0] = hidden_ref[...]
    kv_tiles[...] = jnp.zeros_like(kv_tiles)
    picked[0] = dot(rows_ref[0], hidden_ref[...]).astype(BF16)

    def entry_row(d):
        source = lax.shift_right_logical(d, 2)
        sy = lax.shift_right_logical(source, 2)
        sx = lax.bitwise_and(source, 3)
        return (sx * NY + sy) * 8 + lax.bitwise_and(d, 3)

    d0 = lax.broadcasted_iota(jnp.int32, (HEAD_DIM, 256), 0)
    c1 = lax.broadcasted_iota(jnp.int32, (HEAD_DIM, 256), 1)
    key_place = (entry_row(d0) == c1).astype(F32).astype(BF16)
    r0 = lax.broadcasted_iota(jnp.int32, (256, HEAD_DIM), 0)
    d1 = lax.broadcasted_iota(jnp.int32, (256, HEAD_DIM), 1)
    value_place = (entry_row(d1) + 4 == r0).astype(F32).astype(BF16)
    t0 = lax.broadcasted_iota(jnp.int32, (32, 128), 0)
    k1 = lax.broadcasted_iota(jnp.int32, (32, 128), 1)
    head = lax.shift_right_logical(t0, 3)
    is_value = lax.bitwise_and(lax.shift_right_logical(t0, 2), 1)
    pair = lax.bitwise_and(lax.shift_right_logical(t0, 1), 1)
    tile_place = (16 * is_value + 8 * pair + 2 * head + lax.bitwise_and(t0, 1) == k1).astype(F32).astype(BF16)
    even = lax.bitwise_and(lax.broadcasted_iota(jnp.int32, (ROUTED, 256), 1), 1) == 0
    ones = jnp.ones((ROUTED, 128), BF16)

    pl.semaphore_wait(barrier, len(peers))

    def hid_copy(n):
        return remote(hid.at[n], hid.at[n + 1], hid_send.at[n], hid_recv.at[n + 1], (after, m))

    def picked_copy(n):
        return remote(picked_out.at[n], picked.at[n + 1], picked_send.at[n], picked_recv.at[n + 1], (after, m))

    def tick(n, carry):
        @pl.when(n > 0)
        def _():
            picked_copy(n - 1).wait_recv()

        state = {
            "acc": jnp.zeros((ROUTED, 256), F32),
            "squares": jnp.zeros((ROUTED, 256), F32),
            "routed": jnp.zeros((ROUTED, 256), F32),
        }

        def project(block, source):
            wide = block[...].astype(F32)
            state["squares"] += wide * wide
            state["routed"] += wide * router_ref[source].astype(F32)
            scaled = (wide * gain_ref[source].astype(F32)).astype(BF16)
            state["acc"] += dot(scaled, weight_ref[source])

        finish_rows = gather(picked.at[n], blocks, (ys1, yr1, xs1, xr1, rs1, rr1), project)
        mean = jnp.sum(state["squares"], axis=1, keepdims=True) * (1.0 / (32 * 256))
        inverse_rms = lax.rsqrt(mean + norm_epsilon)
        product = state["acc"] * inverse_rms
        swapped = jnp.where(even, pltpu.roll(product, 255, 1), pltpu.roll(product, 1, 1))
        turned = (product * cos_ref[n] + swapped * sin_ref[n]).astype(BF16)

        tiles = dot_nt(tile_place, turned[:, 128:])
        for k in range(KV_HEADS):
            kv_tiles[k, :, 0:ROUTED] = tiles[8 * k : 8 * k + 8, :]

        def ky_copy(j, source_y):
            return remote(
                kv_tiles.at[lax.div(at_y(j), 2)], kv_all.at[x, source_y], kys.at[j], kyr.at[j], dev(at_y(j), x)
            )

        def kx_copy(j, src_x):
            return remote(kv_all.at[src_x], kv_all.at[src_x], kxs.at[j], kxr.at[j], dev(y, at_x(j)))

        for j in (4, 3, 5, 2, 6, 1, 7):
            ky_copy(j, y).start()
        kv_all[x, y] = kv_tiles[lax.div(y, 2)]
        queries = dot(turned[:, :128], key_place).astype(BF16)
        logits = jnp.sum(state["routed"], axis=1, keepdims=True)
        gate = 1.0 / (1.0 + jnp.exp(-logits))
        for j in range(1, NY):
            ky_copy(j, at_y(-j)).wait_recv()
        for j in (2, 1, 3):
            kx_copy(j, x).start()
        finish_rows()
        for j in range(1, NX):
            kx_copy(j, at_x(-j)).wait_recv()
        kv = kv_all[...].reshape(256, 128).astype(BF16)
        scores = dot(queries, kv) * (1.0 / math.sqrt(HEAD_DIM))
        scores = jnp.where(seen_ref[n] > 0.0, scores, -1e30)
        exponent = jnp.exp(scores - jnp.max(scores, axis=1, keepdims=True))
        weights = (exponent / jnp.sum(exponent, axis=1, keepdims=True)).astype(BF16)
        attended = dot_nt(weights, kv).astype(BF16)
        att[...] = dot(attended, value_place).astype(BF16)
        for j in range(1, NY):
            ky_copy(j, y).wait_send()
        for j in range(1, NX):
            kx_copy(j, x).wait_send()

        state["update"] = jnp.zeros((ROUTED, 256), F32)

        def project_out(block, source):
            state["update"] += dot(block[...], out_weight_ref[source])

        finish_att = gather(att, att_blocks, (ys3, yr3, xs3, xr3, rs3, rr3), project_out)
        new_rows = (picked[n].astype(F32) + gate * state["update"]).astype(BF16)

        @pl.when(n > 0)
        def _():
            hid_copy(n - 1).wait_recv()

        spread = dot_tn(rows_ref[n], new_rows).astype(BF16)
        covered = dot_tn(rows_ref[n], ones)
        covered = jnp.concatenate([covered, covered], axis=1)
        result = jnp.where(covered > 0.5, spread.astype(F32), hid[n].astype(F32)).astype(BF16)
        hid[n] = result

        @pl.when(n < TICKS - 1)
        def _():
            picked_out[n] = dot(next_rows_ref[n], result).astype(BF16)
            picked_copy(n).start()

        hid_copy(n).start()
        finish_att()
        return carry

    lax.fori_loop(0, TICKS, tick, 0)
    hid_copy(TICKS - 1).wait_recv()
    o_ref[...] = hid[TICKS]

    def drain(n, carry):
        hid_copy(n).wait_send()

        @pl.when(n < TICKS - 1)
        def _():
            picked_copy(n).wait_send()

        return carry

    lax.fori_loop(0, TICKS, drain, 0)


def on_device(hidden_in, positions, routed_rows, gain, router, w_query, w_key, w_value, w_out):
    sections = lax.axis_size("section")
    s = lax.axis_index("section")
    m = lax.axis_index("mp")
    tokens, width = hidden_in.shape[1:]
    peers = NX * NY
    token_rows = lax.dynamic_index_in_dim(routed_rows, s, 1, keepdims=False)
    after_rows = lax.dynamic_index_in_dim(routed_rows, (s + 1) % sections, 1, keepdims=False)
    after_rows = jnp.concatenate([after_rows[1:], after_rows[:1]], axis=0)
    token = jnp.arange(tokens, dtype=jnp.int32)
    hot = token_rows[:, :, None] == token
    rows = hot.astype(BF16)
    next_rows = (after_rows[:, :, None] == token).astype(BF16)
    doubled = jnp.concatenate([positions, positions], axis=0)
    held = lax.dynamic_slice_in_dim(doubled, s + sections - TICKS + 1, TICKS, 0)[::-1]
    row_positions = jnp.sum(jnp.where(hot, held[:, None, :], 0), axis=2)

    column = jnp.arange(256, dtype=jnp.int32)
    key_width = w_key.shape[2]
    is_query = column < HEAD_DIM
    pair = jnp.where(is_query, column // 2, (m * key_width + column - HEAD_DIM) // (2 * KV_HEADS))
    frequency = jnp.exp(pair.astype(F32) * (-2.0 * math.log(rope_base) / HEAD_DIM))
    angles = row_positions.astype(F32)[:, :, None] * frequency
    turns = column < HEAD_DIM + key_width
    cosine = jnp.where(turns, jnp.cos(angles), 1.0)
    sine = jnp.where(turns, jnp.where(column % 2 == 0, -1.0, 1.0) * jnp.sin(angles), 0.0)

    others = jnp.pad(token_rows, ((0, 0), (0, 128 - ROUTED)), constant_values=1 << 20)[:, None, :]
    distance = token_rows[:, :, None] - others
    seen = ((distance >= 0) & (distance <= row_positions[:, :, None])).astype(F32)

    spare = jnp.zeros((w_query.shape[1], 256 - HEAD_DIM - 2 * key_width), BF16)
    weight = jnp.concatenate([w_query[0], w_key[0], w_value[0], spare], axis=1).reshape(peers, 256, 256)
    vmem = pl.BlockSpec(memory_space=pltpu.VMEM)
    dma = pltpu.SemaphoreType.DMA
    sems = [dma((NY,)), dma((NY,)), dma((2 * NY,)), dma((2 * NY,)), dma((NY,)), dma((NY,))]
    out = pl.pallas_call(
        functools.partial(kernel, sections),
        out_shape=jax.ShapeDtypeStruct((tokens, width), BF16),
        in_specs=[vmem] * 10,
        out_specs=vmem,
        scratch_shapes=[
            pltpu.VMEM((TICKS + 1, tokens, width), BF16),
            pltpu.VMEM((TICKS, ROUTED, 256), BF16),
            pltpu.VMEM((TICKS, ROUTED, 256), BF16),
            pltpu.VMEM((peers, ROUTED, 256), BF16),
            pltpu.VMEM((KV_HEADS, 8, 128), F32),
            pltpu.VMEM((NX, NY, 8, 128), F32),
            pltpu.VMEM((ROUTED, HEAD_DIM), BF16),
            pltpu.VMEM((peers, ROUTED, HEAD_DIM), BF16),
            dma((TICKS,)), dma((TICKS + 1,)), dma((TICKS,)), dma((TICKS + 1,)),
            *sems, *sems,
            dma((NY,)), dma((NY,)), dma((NX,)), dma((NX,)),
        ],
        compiler_params=pltpu.CompilerParams(collective_id=0, has_side_effects=True),
    )(
        hidden_in[0],
        weight,
        w_out[0].reshape(peers, HEAD_DIM, 256),
        gain[0].reshape(peers, 1, 256),
        router[0].reshape(peers, 1, 256),
        cosine,
        sine,
        seen,
        rows,
        next_rows,
    )
    return out[None, :, :]


def solution(mesh):
    placed = (
        P("section", None, "mp"),
        P(),
        P(),
        P("section", None),
        P("section", None),
        P("section", None, "mp"),
        P("section", None, "mp"),
        P("section", None, "mp"),
        P("section", None, "mp"),
    )
    return jax.shard_map(
        on_device, mesh=mesh, in_specs=placed, out_specs=P("section", None, "mp"), check_vma=False
    )
```

```python
import functools
import math

import jax
import jax.numpy as jnp
from jax import lax
from jax.experimental import pallas as pl
from jax.experimental.pallas import tpu as pltpu
from jax.sharding import PartitionSpec as P

KV_HEADS = 4
HEAD_DIM = 128
TICKS = 8
GROUP = 8
ROUTED = 48
NX = 4
NY = 8

rope_base = 500000.0
norm_epsilon = 1e-05

MESH = pl.DeviceIdType.MESH
F32 = jnp.float32
BF16 = jnp.bfloat16
CHUNKS = ((0, 4), (4, 8))
ORDER = (0, 1, 7, 2, 6, 3, 5, 4)


def dot(a, b):
    return jnp.dot(a, b, preferred_element_type=F32)


def dot_nt(a, b):
    return lax.dot_general(a, b, (((1,), (1,)), ((), ())), preferred_element_type=F32)


def dot_tn(a, b):
    return lax.dot_general(a, b, (((0,), (0,)), ((), ())), preferred_element_type=F32)


def kernel(
    sections,
    hidden_ref, weight_ref, out_weight_ref, gain_ref, router_ref,
    cos_ref, sin_ref, seen_ref, rows_ref, next_rows_ref,
    o_ref,
    hid, picked, picked_out, blocks, kv_tiles, kv_all, att, att_blocks,
    hid_send, hid_recv, picked_send, picked_recv,
    ys1, yr1, xs1, xr1, rs1, rr1,
    ys3, yr3, xs3, xr3, rs3, rr3,
    kys, kyr, kxs, kxr,
):
    s = lax.axis_index("section")
    m = lax.axis_index("mp")
    x = lax.rem(m, NX)
    y = lax.div(m, NX)
    after = lax.rem(s + 1, sections)
    before = lax.rem(s + sections - 1, sections)

    def at_y(d):
        return lax.rem(y + d + NY, NY)

    def at_x(d):
        return lax.rem(x + d + NX, NX)

    def dev(yy, xx):
        return (s, yy * NX + xx)

    barrier = pltpu.get_barrier_semaphore()
    peers = [dev(at_y(d), x) for d in range(1, NY)] + [dev(y, at_x(d)) for d in range(1, NX)]
    peers += [(after, m), (before, m)]
    for peer in peers:
        pl.semaphore_signal(barrier, inc=1, device_id=peer, device_id_type=MESH)

    def remote(src, dst, send, recv, to):
        return pltpu.make_async_remote_copy(
            src_ref=src, dst_ref=dst, send_sem=send, recv_sem=recv, device_id=to, device_id_type=MESH
        )

    def gather(own, into, sems, consume):
        ys, yr, xs, xr, rs, rr = sems
        right = dev(y, at_x(1))
        left = dev(y, at_x(-1))
        chunks = CHUNKS

        def y_copy(t, dest_x):
            return remote(own, into.at[x, t], ys.at[t], yr.at[t], dev(at_y(ORDER[t]), dest_x))

        def part(c, xx):
            first, last = chunks[c]
            return into.at[xx, pl.ds(first, last - first)]

        def x_copy(c, way, xx):
            to = right if way == 0 else left
            return remote(part(c, xx), part(c, xx), xs.at[2 * c + way], xr.at[2 * c + way], to)

        def r_copy(c, xx):
            to = right if c % 2 == 0 else left
            return remote(part(c, xx), part(c, xx), rs.at[c], rr.at[c], to)

        def use(c, xx):
            for t in range(*chunks[c]):
                consume(into.at[xx, t], at_y(-ORDER[t]) * NX + xx)

        for t in range(1, NY):
            y_copy(t, x).start()
        into[x, 0] = own[...]
        sent = []
        for c in range(len(chunks) + 2):
            if c < len(chunks):
                for t in range(max(chunks[c][0], 1), chunks[c][1]):
                    y_copy(t, x).wait_recv()
                for way in (0, 1):
                    copy = x_copy(c, way, x)
                    copy.start()
                    sent.append(copy)
                use(c, x)
            if 1 <= c <= len(chunks):
                for way, xx in ((0, at_x(-1)), (1, at_x(1))):
                    x_copy(c - 1, way, xx).wait_recv()
                    if (c - 1) % 2 == way:
                        copy = r_copy(c - 1, xx)
                        copy.start()
                        sent.append(copy)
                for xx in (at_x(-1), at_x(1)):
                    use(c - 1, xx)
            if c >= 2:
                r_copy(c - 2, at_x(2)).wait_recv()
                use(c - 2, at_x(2))

        def finish():
            for t in range(1, NY):
                y_copy(t, x).wait_send()
            for copy in sent:
                copy.wait_send()

        return finish

    hid[0] = hidden_ref[...]
    kv_tiles[...] = jnp.zeros_like(kv_tiles)
    picked[0] = dot(rows_ref[0], hidden_ref[...]).astype(BF16)

    def entry_row(d):
        source = lax.shift_right_logical(d, 2)
        sy = lax.shift_right_logical(source, 2)
        sx = lax.bitwise_and(source, 3)
        return (sx * NY + sy) * 8 + lax.bitwise_and(d, 3)

    d0 = lax.broadcasted_iota(jnp.int32, (HEAD_DIM, 256), 0)
    c1 = lax.broadcasted_iota(jnp.int32, (HEAD_DIM, 256), 1)
    key_place = (entry_row(d0) == c1).astype(F32).astype(BF16)
    r0 = lax.broadcasted_iota(jnp.int32, (256, HEAD_DIM), 0)
    d1 = lax.broadcasted_iota(jnp.int32, (256, HEAD_DIM), 1)
    value_place = (entry_row(d1) + 4 == r0).astype(F32).astype(BF16)
    t0 = lax.broadcasted_iota(jnp.int32, (32, 128), 0)
    k1 = lax.broadcasted_iota(jnp.int32, (32, 128), 1)
    head = lax.shift_right_logical(t0, 3)
    is_value = lax.bitwise_and(lax.shift_right_logical(t0, 2), 1)
    pair = lax.bitwise_and(lax.shift_right_logical(t0, 1), 1)
    tile_place = (16 * is_value + 8 * pair + 2 * head + lax.bitwise_and(t0, 1) == k1).astype(F32).astype(BF16)
    even = lax.bitwise_and(lax.broadcasted_iota(jnp.int32, (ROUTED, 256), 1), 1) == 0
    ones = jnp.ones((ROUTED, 128), BF16)

    pl.semaphore_wait(barrier, len(peers))

    def hid_copy(n):
        return remote(hid.at[n], hid.at[n + 1], hid_send.at[n], hid_recv.at[n + 1], (after, m))

    def picked_copy(n):
        return remote(picked_out.at[n], picked.at[n + 1], picked_send.at[n], picked_recv.at[n + 1], (after, m))

    def tick(n, carry):
        @pl.when(n > 0)
        def _():
            picked_copy(n - 1).wait_recv()

        state = {
            "acc": jnp.zeros((ROUTED, 256), F32),
            "squares": jnp.zeros((ROUTED, 256), F32),
            "routed": jnp.zeros((ROUTED, 256), F32),
        }

        def project(block, source):
            wide = block[...].astype(F32)
            state["squares"] += wide * wide
            state["routed"] += wide * router_ref[source].astype(F32)
            scaled = (wide * gain_ref[source].astype(F32)).astype(BF16)
            state["acc"] += dot(scaled, weight_ref[source])

        finish_rows = gather(picked.at[n], blocks, (ys1, yr1, xs1, xr1, rs1, rr1), project)
        mean = jnp.sum(state["squares"], axis=1, keepdims=True) * (1.0 / (32 * 256))
        inverse_rms = lax.rsqrt(mean + norm_epsilon)
        product = state["acc"] * inverse_rms
        swapped = jnp.where(even, pltpu.roll(product, 255, 1), pltpu.roll(product, 1, 1))
        turned = (product * cos_ref[n] + swapped * sin_ref[n]).astype(BF16)

        tiles = dot_nt(tile_place, turned[:, 128:])
        for k in range(KV_HEADS):
            kv_tiles[k, :, 0:ROUTED] = tiles[8 * k : 8 * k + 8, :]

        def ky_copy(j, source_y):
            return remote(
                kv_tiles.at[lax.div(at_y(j), 2)], kv_all.at[x, source_y], kys.at[j], kyr.at[j], dev(at_y(j), x)
            )

        def kx_copy(j, src_x):
            return remote(kv_all.at[src_x], kv_all.at[src_x], kxs.at[j], kxr.at[j], dev(y, at_x(j)))

        for j in (4, 3, 5, 2, 6, 1, 7):
            ky_copy(j, y).start()
        kv_all[x, y] = kv_tiles[lax.div(y, 2)]
        queries = dot(turned[:, :128], key_place).astype(BF16)
        logits = jnp.sum(state["routed"], axis=1, keepdims=True)
        gate = 1.0 / (1.0 + jnp.exp(-logits))
        for j in range(1, NY):
            ky_copy(j, at_y(-j)).wait_recv()
        for j in (2, 1, 3):
            kx_copy(j, x).start()
        finish_rows()
        for j in range(1, NX):
            kx_copy(j, at_x(-j)).wait_recv()
        kv = kv_all[...].reshape(256, 128).astype(BF16)
        scores = dot(queries, kv) * (1.0 / math.sqrt(HEAD_DIM))
        scores = jnp.where(seen_ref[n] > 0.0, scores, -1e30)
        exponent = jnp.exp(scores - jnp.max(scores, axis=1, keepdims=True))
        weights = (exponent / jnp.sum(exponent, axis=1, keepdims=True)).astype(BF16)
        attended = dot_nt(weights, kv).astype(BF16)
        att[...] = dot(attended, value_place).astype(BF16)
        for j in range(1, NY):
            ky_copy(j, y).wait_send()
        for j in range(1, NX):
            kx_copy(j, x).wait_send()

        state["update"] = jnp.zeros((ROUTED, 256), F32)

        def project_out(block, source):
            state["update"] += dot(block[...], out_weight_ref[source])

        finish_att = gather(att, att_blocks, (ys3, yr3, xs3, xr3, rs3, rr3), project_out)
        new_rows = (picked[n].astype(F32) + gate * state["update"]).astype(BF16)

        @pl.when(n > 0)
        def _():
            hid_copy(n - 1).wait_recv()

        spread = dot_tn(rows_ref[n], new_rows).astype(BF16)
        covered = dot_tn(rows_ref[n], ones)
        covered = jnp.concatenate([covered, covered], axis=1)
        result = jnp.where(covered > 0.5, spread.astype(F32), hid[n].astype(F32)).astype(BF16)
        hid[n] = result

        @pl.when(n < TICKS - 1)
        def _():
            picked_out[n] = dot(next_rows_ref[n], result).astype(BF16)
            picked_copy(n).start()

        hid_copy(n).start()
        finish_att()
        return carry

    lax.fori_loop(0, TICKS, tick, 0)
    hid_copy(TICKS - 1).wait_recv()
    o_ref[...] = hid[TICKS]

    def drain(n, carry):
        hid_copy(n).wait_send()

        @pl.when(n < TICKS - 1)
        def _():
            picked_copy(n).wait_send()

        return carry

    lax.fori_loop(0, TICKS, drain, 0)


def on_device(hidden_in, positions, routed_rows, gain, router, w_query, w_key, w_value, w_out):
    sections = lax.axis_size("section")
    s = lax.axis_index("section")
    m = lax.axis_index("mp")
    tokens, width = hidden_in.shape[1:]
    peers = NX * NY
    token_rows = lax.dynamic_index_in_dim(routed_rows, s, 1, keepdims=False)
    after_rows = lax.dynamic_index_in_dim(routed_rows, (s + 1) % sections, 1, keepdims=False)
    after_rows = jnp.concatenate([after_rows[1:], after_rows[:1]], axis=0)
    token = jnp.arange(tokens, dtype=jnp.int32)
    hot = token_rows[:, :, None] == token
    rows = hot.astype(BF16)
    next_rows = (after_rows[:, :, None] == token).astype(BF16)
    doubled = jnp.concatenate([positions, positions], axis=0)
    held = lax.dynamic_slice_in_dim(doubled, s + sections - TICKS + 1, TICKS, 0)[::-1]
    row_positions = jnp.sum(jnp.where(hot, held[:, None, :], 0), axis=2)

    column = jnp.arange(256, dtype=jnp.int32)
    key_width = w_key.shape[2]
    is_query = column < HEAD_DIM
    pair = jnp.where(is_query, column // 2, (m * key_width + column - HEAD_DIM) // (2 * KV_HEADS))
    frequency = jnp.exp(pair.astype(F32) * (-2.0 * math.log(rope_base) / HEAD_DIM))
    angles = row_positions.astype(F32)[:, :, None] * frequency
    turns = column < HEAD_DIM + key_width
    cosine = jnp.where(turns, jnp.cos(angles), 1.0)
    sine = jnp.where(turns, jnp.where(column % 2 == 0, -1.0, 1.0) * jnp.sin(angles), 0.0)

    others = jnp.pad(token_rows, ((0, 0), (0, 128 - ROUTED)), constant_values=1 << 20)[:, None, :]
    distance = token_rows[:, :, None] - others
    seen = ((distance >= 0) & (distance <= row_positions[:, :, None])).astype(F32)

    spare = jnp.zeros((w_query.shape[1], 256 - HEAD_DIM - 2 * key_width), BF16)
    weight = jnp.concatenate([w_query[0], w_key[0], w_value[0], spare], axis=1).reshape(peers, 256, 256)
    vmem = pl.BlockSpec(memory_space=pltpu.VMEM)
    dma = pltpu.SemaphoreType.DMA
    sems = [dma((NY,)), dma((NY,)), dma((2 * NY,)), dma((2 * NY,)), dma((NY,)), dma((NY,))]
    out = pl.pallas_call(
        functools.partial(kernel, sections),
        out_shape=jax.ShapeDtypeStruct((tokens, width), BF16),
        in_specs=[vmem] * 10,
        out_specs=vmem,
        scratch_shapes=[
            pltpu.VMEM((TICKS + 1, tokens, width), BF16),
            pltpu.VMEM((TICKS, ROUTED, 256), BF16),
            pltpu.VMEM((TICKS, ROUTED, 256), BF16),
            pltpu.VMEM((NX, NY, ROUTED, 256), BF16),
            pltpu.VMEM((KV_HEADS, 8, 128), F32),
            pltpu.VMEM((NX, NY, 8, 128), F32),
            pltpu.VMEM((ROUTED, HEAD_DIM), BF16),
            pltpu.VMEM((NX, NY, ROUTED, HEAD_DIM), BF16),
            dma((TICKS,)), dma((TICKS + 1,)), dma((TICKS,)), dma((TICKS + 1,)),
            *sems, *sems,
            dma((NY,)), dma((NY,)), dma((NX,)), dma((NX,)),
        ],
        compiler_params=pltpu.CompilerParams(collective_id=0, has_side_effects=True),
    )(
        hidden_in[0],
        weight,
        w_out[0].reshape(peers, HEAD_DIM, 256),
        gain[0].reshape(peers, 1, 256),
        router[0].reshape(peers, 1, 256),
        cosine,
        sine,
        seen,
        rows,
        next_rows,
    )
    return out[None, :, :]


def solution(mesh):
    placed = (
        P("section", None, "mp"),
        P(),
        P(),
        P("section", None),
        P("section", None),
        P("section", None, "mp"),
        P("section", None, "mp"),
        P("section", None, "mp"),
        P("section", None, "mp"),
    )
    return jax.shard_map(
        on_device, mesh=mesh, in_specs=placed, out_specs=P("section", None, "mp"), check_vma=False
    )
```

```python
import functools
import math

import jax
import jax.numpy as jnp
from jax import lax
from jax.experimental import pallas as pl
from jax.experimental.pallas import tpu as pltpu
from jax.sharding import PartitionSpec as P

KV_HEADS = 4
HEAD_DIM = 128
TICKS = 8
GROUP = 8
ROUTED = 48
NX = 4
NY = 8

rope_base = 500000.0
norm_epsilon = 1e-05

MESH = pl.DeviceIdType.MESH
F32 = jnp.float32
BF16 = jnp.bfloat16
ORDER = (0, 1, 7, 2, 6, 3, 5, 4)


def dot(a, b):
    return jnp.dot(a, b, preferred_element_type=F32)


def dot_nt(a, b):
    return lax.dot_general(a, b, (((1,), (1,)), ((), ())), preferred_element_type=F32)


def dot_tn(a, b):
    return lax.dot_general(a, b, (((0,), (0,)), ((), ())), preferred_element_type=F32)


def kernel(
    sections,
    hidden_ref, weight_ref, out_weight_ref, gain_ref, router_ref,
    cos_ref, sin_ref, seen_ref, rows_ref, next_rows_ref,
    o_ref,
    hid, picked, picked_out, blocks, kv_tiles, kv_all, att, att_blocks,
    hid_send, hid_recv, picked_send, picked_recv,
    ys1, yr1, xs1, xr1, rs1, rr1,
    ys3, yr3, xs3, xr3, rs3, rr3,
    kys, kyr, kxs, kxr,
):
    s = lax.axis_index("section")
    m = lax.axis_index("mp")
    x = lax.rem(m, NX)
    y = lax.div(m, NX)
    after = lax.rem(s + 1, sections)
    before = lax.rem(s + sections - 1, sections)

    def at_y(d):
        return lax.rem(y + d + NY, NY)

    def at_x(d):
        return lax.rem(x + d + NX, NX)

    def dev(yy, xx):
        return (s, yy * NX + xx)

    barrier = pltpu.get_barrier_semaphore()
    peers = [dev(at_y(d), x) for d in range(1, NY)] + [dev(y, at_x(d)) for d in range(1, NX)]
    peers += [(after, m), (before, m)]
    for peer in peers:
        pl.semaphore_signal(barrier, inc=1, device_id=peer, device_id_type=MESH)

    def remote(src, dst, send, recv, to):
        return pltpu.make_async_remote_copy(
            src_ref=src, dst_ref=dst, send_sem=send, recv_sem=recv, device_id=to, device_id_type=MESH
        )

    def gather(own, into, sems, consume, chunks, direct):
        ys, yr, xs, xr, rs, rr = sems
        right = dev(y, at_x(1))
        left = dev(y, at_x(-1))

        def y_copy(t, dest_x):
            return remote(own, into.at[x, t], ys.at[t], yr.at[t], dev(at_y(ORDER[t]), dest_x))

        def part(c, xx):
            first, last = chunks[c]
            return into.at[xx, pl.ds(first, last - first)]

        def x_copy(c, way, xx):
            to = right if way == 0 else left
            return remote(part(c, xx), part(c, xx), xs.at[2 * c + way], xr.at[2 * c + way], to)

        def r_copy(c, xx):
            to = right if c % 2 == 0 else left
            if direct:
                to = dev(y, at_x(2))
            return remote(part(c, xx), part(c, xx), rs.at[c], rr.at[c], to)

        def use(c, xx):
            for t in range(*chunks[c]):
                consume(into.at[xx, t], at_y(-ORDER[t]) * NX + xx)

        for t in range(1, NY):
            y_copy(t, x).start()
        into[x, 0] = own[...]
        sent = []
        for c in range(len(chunks) + 2):
            if c < len(chunks):
                for t in range(max(chunks[c][0], 1), chunks[c][1]):
                    y_copy(t, x).wait_recv()
                if direct:
                    copy = r_copy(c, x)
                    copy.start()
                    sent.append(copy)
                for way in (0, 1):
                    copy = x_copy(c, way, x)
                    copy.start()
                    sent.append(copy)
                use(c, x)
            if 1 <= c <= len(chunks):
                for way, xx in ((0, at_x(-1)), (1, at_x(1))):
                    x_copy(c - 1, way, xx).wait_recv()
                    if not direct and (c - 1) % 2 == way:
                        copy = r_copy(c - 1, xx)
                        copy.start()
                        sent.append(copy)
                for xx in (at_x(-1), at_x(1)):
                    use(c - 1, xx)
            if c >= 2:
                r_copy(c - 2, at_x(2)).wait_recv()
                use(c - 2, at_x(2))

        def finish():
            for t in range(1, NY):
                y_copy(t, x).wait_send()
            for copy in sent:
                copy.wait_send()

        return finish

    hid[0] = hidden_ref[...]
    kv_tiles[...] = jnp.zeros_like(kv_tiles)
    picked[0] = dot(rows_ref[0], hidden_ref[...]).astype(BF16)

    def entry_row(d):
        source = lax.shift_right_logical(d, 2)
        sy = lax.shift_right_logical(source, 2)
        sx = lax.bitwise_and(source, 3)
        return (sx * NY + sy) * 8 + lax.bitwise_and(d, 3)

    d0 = lax.broadcasted_iota(jnp.int32, (HEAD_DIM, 256), 0)
    c1 = lax.broadcasted_iota(jnp.int32, (HEAD_DIM, 256), 1)
    key_place = (entry_row(d0) == c1).astype(F32).astype(BF16)
    r0 = lax.broadcasted_iota(jnp.int32, (256, HEAD_DIM), 0)
    d1 = lax.broadcasted_iota(jnp.int32, (256, HEAD_DIM), 1)
    value_place = (entry_row(d1) + 4 == r0).astype(F32).astype(BF16)
    t0 = lax.broadcasted_iota(jnp.int32, (32, 128), 0)
    k1 = lax.broadcasted_iota(jnp.int32, (32, 128), 1)
    head = lax.shift_right_logical(t0, 3)
    is_value = lax.bitwise_and(lax.shift_right_logical(t0, 2), 1)
    pair = lax.bitwise_and(lax.shift_right_logical(t0, 1), 1)
    tile_place = (16 * is_value + 8 * pair + 2 * head + lax.bitwise_and(t0, 1) == k1).astype(F32).astype(BF16)
    even = lax.bitwise_and(lax.broadcasted_iota(jnp.int32, (ROUTED, 256), 1), 1) == 0
    ones = jnp.ones((ROUTED, 128), BF16)

    pl.semaphore_wait(barrier, len(peers))

    def hid_copy(n):
        return remote(hid.at[n], hid.at[n + 1], hid_send.at[n], hid_recv.at[n + 1], (after, m))

    def picked_copy(n):
        return remote(picked_out.at[n], picked.at[n + 1], picked_send.at[n], picked_recv.at[n + 1], (after, m))

    def tick(n, carry):
        @pl.when(n > 0)
        def _():
            picked_copy(n - 1).wait_recv()

        state = {
            "acc": jnp.zeros((ROUTED, 256), F32),
            "squares": jnp.zeros((ROUTED, 256), F32),
            "routed": jnp.zeros((ROUTED, 256), F32),
        }

        def project(block, source):
            wide = block[...].astype(F32)
            state["squares"] += wide * wide
            state["routed"] += wide * router_ref[source].astype(F32)
            scaled = (wide * gain_ref[source].astype(F32)).astype(BF16)
            state["acc"] += dot(scaled, weight_ref[source])

        finish_rows = gather(picked.at[n], blocks, (ys1, yr1, xs1, xr1, rs1, rr1), project, ((0, 4), (4, 8)), True)
        mean = jnp.sum(state["squares"], axis=1, keepdims=True) * (1.0 / (32 * 256))
        inverse_rms = lax.rsqrt(mean + norm_epsilon)
        product = state["acc"] * inverse_rms
        swapped = jnp.where(even, pltpu.roll(product, 255, 1), pltpu.roll(product, 1, 1))
        turned = (product * cos_ref[n] + swapped * sin_ref[n]).astype(BF16)

        tiles = dot_nt(tile_place, turned[:, 128:])
        for k in range(KV_HEADS):
            kv_tiles[k, :, 0:ROUTED] = tiles[8 * k : 8 * k + 8, :]

        def ky_copy(j, source_y):
            return remote(
                kv_tiles.at[lax.div(at_y(j), 2)], kv_all.at[x, source_y], kys.at[j], kyr.at[j], dev(at_y(j), x)
            )

        def kx_copy(j, src_x):
            return remote(kv_all.at[src_x], kv_all.at[src_x], kxs.at[j], kxr.at[j], dev(y, at_x(j)))

        for j in (4, 3, 5, 2, 6, 1, 7):
            ky_copy(j, y).start()
        kv_all[x, y] = kv_tiles[lax.div(y, 2)]
        queries = dot(turned[:, :128], key_place).astype(BF16)
        logits = jnp.sum(state["routed"], axis=1, keepdims=True)
        gate = 1.0 / (1.0 + jnp.exp(-logits))
        for j in range(1, NY):
            ky_copy(j, at_y(-j)).wait_recv()
        for j in (2, 1, 3):
            kx_copy(j, x).start()
        finish_rows()
        for j in range(1, NX):
            kx_copy(j, at_x(-j)).wait_recv()
        kv = kv_all[...].reshape(256, 128).astype(BF16)
        scores = dot(queries, kv) * (1.0 / math.sqrt(HEAD_DIM))
        scores = jnp.where(seen_ref[n] > 0.0, scores, -1e30)
        exponent = jnp.exp(scores - jnp.max(scores, axis=1, keepdims=True))
        weights = (exponent / jnp.sum(exponent, axis=1, keepdims=True)).astype(BF16)
        attended = dot_nt(weights, kv).astype(BF16)
        att[...] = dot(attended, value_place).astype(BF16)
        for j in range(1, NY):
            ky_copy(j, y).wait_send()
        for j in range(1, NX):
            kx_copy(j, x).wait_send()

        state["update"] = jnp.zeros((ROUTED, 256), F32)

        def project_out(block, source):
            state["update"] += dot(block[...], out_weight_ref[source])

        finish_att = gather(att, att_blocks, (ys3, yr3, xs3, xr3, rs3, rr3), project_out, ((0, 4), (4, 8)), True)
        new_rows = (picked[n].astype(F32) + gate * state["update"]).astype(BF16)

        @pl.when(n > 0)
        def _():
            hid_copy(n - 1).wait_recv()

        spread = dot_tn(rows_ref[n], new_rows).astype(BF16)
        covered = dot_tn(rows_ref[n], ones)
        covered = jnp.concatenate([covered, covered], axis=1)
        result = jnp.where(covered > 0.5, spread.astype(F32), hid[n].astype(F32)).astype(BF16)
        hid[n] = result

        @pl.when(n < TICKS - 1)
        def _():
            picked_out[n] = dot(next_rows_ref[n], result).astype(BF16)
            picked_copy(n).start()

        hid_copy(n).start()
        finish_att()
        return carry

    lax.fori_loop(0, TICKS, tick, 0)
    hid_copy(TICKS - 1).wait_recv()
    o_ref[...] = hid[TICKS]

    def drain(n, carry):
        hid_copy(n).wait_send()

        @pl.when(n < TICKS - 1)
        def _():
            picked_copy(n).wait_send()

        return carry

    lax.fori_loop(0, TICKS, drain, 0)


def on_device(hidden_in, positions, routed_rows, gain, router, w_query, w_key, w_value, w_out):
    sections = lax.axis_size("section")
    s = lax.axis_index("section")
    m = lax.axis_index("mp")
    tokens, width = hidden_in.shape[1:]
    peers = NX * NY
    token_rows = lax.dynamic_index_in_dim(routed_rows, s, 1, keepdims=False)
    after_rows = lax.dynamic_index_in_dim(routed_rows, (s + 1) % sections, 1, keepdims=False)
    after_rows = jnp.concatenate([after_rows[1:], after_rows[:1]], axis=0)
    token = jnp.arange(tokens, dtype=jnp.int32)
    hot = token_rows[:, :, None] == token
    rows = hot.astype(BF16)
    next_rows = (after_rows[:, :, None] == token).astype(BF16)
    doubled = jnp.concatenate([positions, positions], axis=0)
    held = lax.dynamic_slice_in_dim(doubled, s + sections - TICKS + 1, TICKS, 0)[::-1]
    row_positions = jnp.sum(jnp.where(hot, held[:, None, :], 0), axis=2)

    column = jnp.arange(256, dtype=jnp.int32)
    key_width = w_key.shape[2]
    is_query = column < HEAD_DIM
    pair = jnp.where(is_query, column // 2, (m * key_width + column - HEAD_DIM) // (2 * KV_HEADS))
    frequency = jnp.exp(pair.astype(F32) * (-2.0 * math.log(rope_base) / HEAD_DIM))
    angles = row_positions.astype(F32)[:, :, None] * frequency
    turns = column < HEAD_DIM + key_width
    cosine = jnp.where(turns, jnp.cos(angles), 1.0)
    sine = jnp.where(turns, jnp.where(column % 2 == 0, -1.0, 1.0) * jnp.sin(angles), 0.0)

    others = jnp.pad(token_rows, ((0, 0), (0, 128 - ROUTED)), constant_values=1 << 20)[:, None, :]
    distance = token_rows[:, :, None] - others
    seen = ((distance >= 0) & (distance <= row_positions[:, :, None])).astype(F32)

    spare = jnp.zeros((w_query.shape[1], 256 - HEAD_DIM - 2 * key_width), BF16)
    weight = jnp.concatenate([w_query[0], w_key[0], w_value[0], spare], axis=1).reshape(peers, 256, 256)
    vmem = pl.BlockSpec(memory_space=pltpu.VMEM)
    dma = pltpu.SemaphoreType.DMA
    sems = [dma((NY,)), dma((NY,)), dma((2 * NY,)), dma((2 * NY,)), dma((NY,)), dma((NY,))]
    out = pl.pallas_call(
        functools.partial(kernel, sections),
        out_shape=jax.ShapeDtypeStruct((tokens, width), BF16),
        in_specs=[vmem] * 10,
        out_specs=vmem,
        scratch_shapes=[
            pltpu.VMEM((TICKS + 1, tokens, width), BF16),
            pltpu.VMEM((TICKS, ROUTED, 256), BF16),
            pltpu.VMEM((TICKS, ROUTED, 256), BF16),
            pltpu.VMEM((NX, NY, ROUTED, 256), BF16),
            pltpu.VMEM((KV_HEADS, 8, 128), F32),
            pltpu.VMEM((NX, NY, 8, 128), F32),
            pltpu.VMEM((ROUTED, HEAD_DIM), BF16),
            pltpu.VMEM((NX, NY, ROUTED, HEAD_DIM), BF16),
            dma((TICKS,)), dma((TICKS + 1,)), dma((TICKS,)), dma((TICKS + 1,)),
            *sems, *sems,
            dma((NY,)), dma((NY,)), dma((NX,)), dma((NX,)),
        ],
        compiler_params=pltpu.CompilerParams(collective_id=0, has_side_effects=True),
    )(
        hidden_in[0],
        weight,
        w_out[0].reshape(peers, HEAD_DIM, 256),
        gain[0].reshape(peers, 1, 256),
        router[0].reshape(peers, 1, 256),
        cosine,
        sine,
        seen,
        rows,
        next_rows,
    )
    return out[None, :, :]


def solution(mesh):
    placed = (
        P("section", None, "mp"),
        P(),
        P(),
        P("section", None),
        P("section", None),
        P("section", None, "mp"),
        P("section", None, "mp"),
        P("section", None, "mp"),
        P("section", None, "mp"),
    )
    return jax.shard_map(
        on_device, mesh=mesh, in_specs=placed, out_specs=P("section", None, "mp"), check_vma=False
    )
```
